32 devices in a mesh: groups: 2 (over y), band: 8 (over z, x), sub: 2 (over core).
Axes of the slice: x: 2, y: 2, z: 4, core: 2. Of those that a mesh axis runs over, the one named last changes fastest.
Arguments:
- features: bfloat16 [49152, 128], P(('groups', 'band', 'sub')), parts along dimension 0, may hold values from -6 to 6
- near_off: int32 [768, 16], P(('groups', 'band', 'sub')), parts along dimension 0, may hold values from 0 to 16
- near_val: bfloat16 [49152, 1024], P(('groups', 'band', 'sub')), parts along dimension 0, may hold values from -6 to 6
- far_slot: int32 [768, 16], P(('groups', 'band', 'sub')), parts along dimension 0, may hold values from 0 to 31, as said below
- far_val: bfloat16 [49152, 1024], P(('groups', 'band', 'sub')), parts along dimension 0, may hold values from -6 to 6
- send_blk: int32 [32, 16, 2], P(('groups', 'band', 'sub')), parts along dimension 0, may hold values from -1 to 23, as said below
Outputs:
- spectral: bfloat16 [49152, 128], P(('groups', 'band', 'sub')), parts along dimension 0
The draws below stay inside these ranges and needn't reach their ends.
There are 2 independent parts, one for each index of `groups`. The reference program is written for one: setup_inputs(seed, part) draws one part's arguments, and reference() takes and returns one part's arrays. A program takes and returns all parts, laid end to end along the dimension named above; each array names one. Nothing has to cross between parts.
Inputs may be any that keep to these rules, and one draw needn't show every extreme that they name: `send_blk`: slots of a pair are filled from the first; each (provider, reader) pair has 1 to 2 filled slots holding different row blocks. `far_slot`: each entry names a filled slot of its device's reads: provider slot // 2, slot slot % 2; every filled slot for a device is named by some entry of that device.
All inputs are finite; a program needn't handle non-finite values.
Results may differ from the reference program's by a relative error of at most 0.0038.
Values may be sent and summed in bfloat16 or wider, within the bound.
A program may use at most 128 MiB of HBM per device.

```python
import math
import jax
import jax.numpy as jnp
from jax import lax

F = 128
BLK = 64
BR = 24
HB = 8
NPR = 16
FPR = 16
CAP = 2
ORDER = 3
PEERS = 16
NB = 384
NV = 24576
N_BAND = 8
N_SUB = 2


def links_table(key):
    base_key = jax.random.fold_in(key, 11)
    key_count, key_start, key_order, key_hubs = jax.random.split(base_key, 4)
    hubs = jax.random.randint(key_hubs, (PEERS,), 0, 4) == 0
    counts = jnp.where(hubs[None, :], CAP, 1 + jax.random.randint(key_count, (PEERS, PEERS), 0, CAP))
    counts = counts.at[:, PEERS - 1].set(CAP)
    counts = counts.at[0, 1].set(1)
    start = jax.random.randint(key_start, (PEERS, PEERS), 0, BR)
    start = start.at[0, 0].set(BR - 1)
    position = jnp.arange(CAP, dtype=jnp.int32)
    chosen = (start[:, :, None] + position[None, None, :]) % BR
    filled = position[None, None, :] < counts[:, :, None]
    readers = jnp.where(filled, chosen, -1).astype(jnp.int32)
    return (counts.astype(jnp.int32), readers, key_order)


def draw_send_blk(key, part):
    counts, readers, key_order = links_table(key)
    return jnp.transpose(readers, (1, 0, 2)).astype(jnp.int32)


def draw_far_slot(key, part):
    counts, readers, key_order = links_table(key)
    entries = BR * FPR
    entry = jnp.arange(entries, dtype=jnp.int32)
    slot = entry % (PEERS * CAP)
    source = slot // CAP
    position = slot % CAP
    usable = position[None, :] < counts[:, source]
    slots = jnp.where(usable, slot[None, :], (source * CAP)[None, :])
    order_keys = jax.random.split(key_order, PEERS)
    orders = jax.vmap(lambda single: jax.random.permutation(single, entries))(order_keys)
    shuffled = jnp.take_along_axis(slots, orders.astype(jnp.int32), axis=1)
    return shuffled.reshape(PEERS * BR, FPR).astype(jnp.int32)


def place_ends(values, stream_key, low, high):
    dims = values.shape
    index_at = [jax.random.randint(jax.random.fold_in(stream_key, axis), (), 0, dims[axis]) for axis in range(len(dims))]
    values = values.at[tuple(index_at)].set(low)
    longest = dims.index(max(dims))
    index_at[longest] = (index_at[longest] + 1) % dims[longest]
    return values.at[tuple(index_at)].set(high)


def block_scale(rng, shape, cuts, least, largest):
    def one(dim, parts):
        heights = jax.random.uniform(jax.random.fold_in(jax.random.fold_in(rng, 6), dim), (parts,), jnp.float32, least / len(cuts), largest / len(cuts))
        return jnp.repeat(jnp.exp(heights), shape[dim] // parts).reshape((-1,) + (1,) * (len(shape) - dim - 1))

    factor_of = one(*cuts[0])
    for cut in cuts[1:]:
        factor_of = factor_of * one(*cut)
    return factor_of


def gaussian(stream_key, dims, deviation, reach, pieces=(), kind=jnp.bfloat16):
    drawn = deviation * jax.random.normal(stream_key, dims, jnp.float32)
    if pieces:
        drawn = drawn * block_scale(stream_key, dims, pieces, -0.22, 0.18)
    return jnp.clip(drawn, -reach, reach).astype(kind)


def setup_inputs(seed: int = 0, part: int = 0) -> dict:
    key_of = jax.random.split(jax.random.key(seed), 7)
    part_keys = jax.random.split(jax.random.fold_in(key_of[6], part), 7)
    return {
        "features": gaussian(part_keys[0], (NV, F), 1.0, 6.0, ((0, 16),)),
        "near_off": place_ends(jax.random.randint(part_keys[1], (NB, NPR), 0, 2 * HB + 1), jax.random.fold_in(part_keys[1], 1), 0, 2 * HB).astype(jnp.int32),
        "near_val": gaussian(part_keys[2], (NV, NPR * BLK), 1.0, 6.0, ((0, 16),)),
        "far_slot": draw_far_slot(jax.random.fold_in(jax.random.fold_in(key_of[6], part), 71), part),
        "far_val": gaussian(part_keys[4], (NV, FPR * BLK), 1.0, 6.0, ((0, 16),)),
        "send_blk": draw_send_blk(jax.random.fold_in(jax.random.fold_in(key_of[6], part), 71), part),
    }


def bessel_value(order, theta):
    total = 0.0
    for term in range(30):
        total += (theta / 2.0) ** (2 * term + order) / (math.factorial(term) * math.factorial(term + order))
    return total

def coefficients(count):
    values = [bessel_value(0, 1.5)]
    for order in range(1, count + 1):
        values.append(2.0 * (-1.0) ** order * bessel_value(order, 1.5))
    return values

def reference(features, near_off, near_val, far_slot, far_val, send_blk):
    peers = N_BAND * N_SUB
    total_rows, width = features.shape
    nblocks = total_rows // BLK
    squares = lax.optimization_barrier(jnp.sum(jnp.square(near_val.astype(jnp.float32)), axis=1)) + lax.optimization_barrier(jnp.sum(jnp.square(far_val.astype(jnp.float32)), axis=1))
    inv_norm = lax.rsqrt(squares + 1e-06)
    rowblock = jnp.arange(nblocks, dtype=jnp.int32)
    near_index = (rowblock[:, None] + near_off).astype(jnp.int32)
    device = rowblock // BR
    source = far_slot // CAP
    position = far_slot % CAP
    far_block = send_blk[source, device[:, None], position]
    far_index = (source * BR + far_block).astype(jnp.int32)
    near_values = near_val.reshape(peers, BR, BLK, NPR * BLK)
    far_values = far_val.reshape(peers, BR, BLK, FPR * BLK)
    near_index = near_index.reshape(peers, BR, NPR)
    far_index = far_index.reshape(peers, BR, FPR)

    def operate(field):
        tiles = field.reshape(nblocks, BLK, width)
        margin = jnp.zeros((HB, BLK, width), field.dtype)
        padded = jnp.concatenate([margin, tiles, margin], axis=0)

        def one_device(items):
            near_v, far_v, near_i, far_i = items
            near_rows = padded[near_i].reshape(BR, NPR * BLK, width).astype(jnp.float32)
            far_rows = tiles[far_i].reshape(BR, FPR * BLK, width).astype(jnp.float32)
            first = jnp.einsum('rik,rkf->rif', near_v.astype(jnp.float32), near_rows)
            second = jnp.einsum('rik,rkf->rif', far_v.astype(jnp.float32), far_rows)
            return first + second
        summed = lax.map(one_device, (near_values, far_values, near_index, far_index)).reshape(total_rows, width)
        return summed * inv_norm[:, None] - 0.2 * field.astype(jnp.float32)
    coef = coefficients(ORDER)
    previous = features
    accum = coef[0] * features.astype(jnp.float32)
    result = operate(features)
    accum = accum + coef[1] * result
    current = result.astype(jnp.bfloat16)
    for order in range(2, ORDER + 1):
        result = 2.0 * operate(current) - previous.astype(jnp.float32)
        accum = accum + coef[order] * result
        previous = current
        current = result.astype(jnp.bfloat16)
    return accum.astype(jnp.bfloat16)
```

```python
import functools
import math

import jax
import jax.numpy as jnp
from jax import lax
from jax.experimental import pallas as pl
from jax.experimental.pallas import tpu as pltpu
from jax.sharding import PartitionSpec as P

HB = 8
ORDER = 3
CHUNKS = 4
UNROLL = 12
HALVES = 2
QUARTERS = 4
RELAYS = 4
MESH = pl.DeviceIdType.MESH


def bessel_value(order, theta):
    total = 0.0
    for term in range(30):
        total += (theta / 2.0) ** (2 * term + order) / (
            math.factorial(term) * math.factorial(term + order)
        )
    return total


def coefficients(count):
    values = [bessel_value(0, 1.5)]
    for order in range(1, count + 1):
        values.append(2.0 * (-1.0) ** order * bessel_value(order, 1.5))
    return values


def kernel(
    bands,
    subs,
    feat_hbm,
    near_off,
    far_slot,
    send_blk,
    near_hbm,
    far_hbm,
    out_ref,
    feat_ref,
    near_s,
    far_s,
    near_p,
    far_p,
    own,
    above,
    below,
    outgoing,
    arrived,
    inv,
    partial,
    accum,
    feat_sem,
    load_sem,
    ready,
    send_sem,
    recv_sem,
    halo_send,
    halo_recv,
    relay,
    relay_send,
    relay_recv,
    relay_done,
):
    peers = bands * subs
    blocks, block, width = feat_ref.shape
    near_count = near_off.shape[0]
    far_count = far_slot.shape[0]
    capacity = send_blk.shape[1]
    me = lax.axis_index("band") * subs + lax.axis_index("sub")
    coef = coefficients(ORDER)
    step = blocks // CHUNKS
    short = block // HALVES
    stages = ORDER * HALVES
    left = lax.broadcasted_iota(jnp.int32, (short, width), 1) < width // 2
    even = lax.broadcasted_iota(jnp.int32, (block, 128), 1) % (2 * short) < short

    def swap(values):
        return pltpu.roll(values, width // 2, 1)

    def exchange(first, second):
        return jnp.where(left, first, swap(second)), jnp.where(left, swap(first), second)

    def where(peer):
        return {"band": peer // subs, "sub": peer % subs}

    def loads(part):
        source, target = ((near_hbm, near_s), (far_hbm, far_s))[part]
        return [
            pltpu.make_async_copy(
                source.at[pl.ds(c * step, step)],
                target.at[pl.ds(c * step, step)],
                load_sem.at[part, c],
            )
            for c in range(CHUNKS)
        ]

    barrier = pltpu.get_barrier_semaphore()

    def greet(peer, carry):
        pl.semaphore_signal(barrier, inc=1, device_id=where(peer), device_id_type=MESH)
        return carry

    lax.fori_loop(me + 1, peers, greet, 0)
    features = pltpu.make_async_copy(feat_hbm, feat_ref, feat_sem)
    features.start()
    for part in range(2):
        for copy in loads(part):
            copy.start()

    @pl.when(me > 0)
    def _():
        pl.semaphore_wait(barrier, me)

    quarter = peers // QUARTERS

    def admit(peer, carry):
        pl.semaphore_signal(
            ready.at[me // quarter], inc=1, device_id=where(peer), device_id_type=MESH
        )
        return carry

    lax.fori_loop(0, me, admit, 0)
    features.wait()

    def pack(g, carry):
        field = feat_ref[g].astype(jnp.float32)
        for h, packed in enumerate(exchange(field[:short], field[short:])):
            packed = packed.astype(jnp.bfloat16)
            own[h][g] = packed
            above[h][HB + g] = packed
            below[h][g] = packed
        return carry

    lax.fori_loop(0, blocks, pack, 0, unroll=4)

    @pl.when(me == 0)
    def _():
        for k in range(stages):
            above[k][0:HB] = jnp.zeros((HB, short, width), jnp.bfloat16)

    @pl.when(me == peers - 1)
    def _():
        for k in range(stages):
            below[k][blocks:] = jnp.zeros((HB, short, width), jnp.bfloat16)

    def halo_up(k):
        return pltpu.make_async_remote_copy(
            src_ref=own[k].at[pl.ds(blocks - HB, HB)],
            dst_ref=above[k].at[pl.ds(0, HB)],
            send_sem=halo_send.at[k, 0],
            recv_sem=halo_recv.at[k, 0],
            device_id=where((me + 1) % peers),
            device_id_type=MESH,
        )

    def halo_down(k):
        return pltpu.make_async_remote_copy(
            src_ref=own[k].at[pl.ds(0, HB)],
            dst_ref=below[k].at[pl.ds(blocks, HB)],
            send_sem=halo_send.at[k, 1],
            recv_sem=halo_recv.at[k, 1],
            device_id=where((me + peers - 1) % peers),
            device_id_type=MESH,
        )

    def await_ready(q):
        late = jnp.clip((q + 1) * quarter - 1 - me, 0, quarter)

        @pl.when(late > 0)
        def _():
            pl.semaphore_wait(ready.at[q], late)

    low = me < peers // 2

    def span(k, q):
        def one(j, carry):
            peer = q * quarter + j

            @pl.when(peer != me)
            def _():
                for c in range(capacity):
                    block_index = jnp.maximum(send_blk[0, c, peer], 0)
                    outgoing[k][peer * capacity + c] = own[k][block_index]
                pltpu.make_async_remote_copy(
                    src_ref=outgoing[k].at[pl.ds(peer * capacity, capacity)],
                    dst_ref=arrived[k].at[pl.ds(me * capacity, capacity)],
                    send_sem=send_sem.at[k],
                    recv_sem=recv_sem.at[k],
                    device_id=where(peer),
                    device_id_type=MESH,
                ).start()

            return carry

        lax.fori_loop(0, quarter, one, 0)

    middle = peers // 2
    share = HB // RELAYS
    up_base = middle - RELAYS
    is_up_relay = (me >= up_base) & (me < middle - 1)
    is_down_relay = (me > middle) & (me < middle + RELAYS)

    def hand(k, first, sem, peer, i):
        return pltpu.make_async_remote_copy(
            src_ref=own[k].at[pl.ds(first + i * share, share)],
            dst_ref=relay[k],
            send_sem=sem,
            recv_sem=relay_recv.at[k],
            device_id=where(peer),
            device_id_type=MESH,
        )

    def direct(k, side):
        i = (1 - side) * (RELAYS - 1)
        source = (1 - side) * (blocks - HB) + i * share
        target = (above, below)[side][k].at[pl.ds(side * blocks + i * share, share)]
        return pltpu.make_async_remote_copy(
            src_ref=own[k].at[pl.ds(source, share)],
            dst_ref=target,
            send_sem=halo_send.at[k, side],
            recv_sem=halo_recv.at[k, side],
            device_id=where(middle - side),
            device_id_type=MESH,
        )

    def hand_up(k):
        @pl.when(me == middle - 1)
        def _():
            for i in range(RELAYS - 1):
                hand(k, blocks - HB, halo_send.at[k, 0], up_base + i, i).start()

    def hand_down(k):
        @pl.when(me == middle)
        def _():
            for i in range(1, RELAYS):
                hand(k, 0, halo_send.at[k, 1], middle + i, i).start()

    def forward_copy(k, side):
        i = (me - middle) if side else (me - up_base)
        return pltpu.make_async_remote_copy(
            src_ref=relay[k],
            dst_ref=(above, below)[side][k].at[pl.ds(side * blocks + i * share, share)],
            send_sem=relay_send.at[k],
            recv_sem=relay_done.at[k],
            device_id=where(middle - side),
            device_id_type=MESH,
        )

    def forward(k):
        for side, mine in enumerate((is_up_relay, is_down_relay)):

            @pl.when(mine)
            def _():
                pltpu.make_async_copy(relay[k], relay[k], relay_recv.at[k]).wait()
                forward_copy(k, side).start()

    def send_down(k):
        @pl.when(me == middle)
        def _():
            direct(k, 1).start()

        @pl.when((me > 0) & (me != middle))
        def _():
            halo_down(k).start()

    def send_up(k):
        @pl.when(me == middle - 1)
        def _():
            direct(k, 0).start()

        @pl.when((me < peers - 1) & (me != middle - 1))
        def _():
            halo_up(k).start()

    def keep(k):
        for c in range(capacity):
            block_index = jnp.maximum(send_blk[0, c, me], 0)
            arrived[k][me * capacity + c] = own[k][block_index]

    def send_first():
        @pl.when(low)
        def _():
            for q in (0, 1):
                await_ready(q)
            for k in range(HALVES):
                hand_up(k)
            for q in (0, 1):
                span(0, q)
            for q in (2, 3):
                await_ready(q)
                span(0, q)
            for k in range(HALVES):
                send_up(k)
                send_down(k)
            for q in (2, 3, 0, 1):
                span(1, q)

        @pl.when(jnp.logical_not(low))
        def _():
            for k in range(HALVES):
                span(k, 0)
                span(k, 1)
                send_down(k)
            await_ready(2)
            for k in range(HALVES):
                hand_down(k)
            span(0, 2)
            await_ready(3)
            span(0, 3)
            for k in range(HALVES):
                send_up(k)
            for q in (2, 3):
                span(1, q)

        for k in range(HALVES):
            keep(k)

    def send_all(k):
        hand_up(k)
        hand_down(k)
        send_down(k)
        send_up(k)

        @pl.when(low)
        def _():
            span(k, 2)
            span(k, 3)

        @pl.when(jnp.logical_not(low))
        def _():
            span(k, 0)
            span(k, 1)

        @pl.when(low)
        def _():
            span(k, 0)
            span(k, 1)

        @pl.when(jnp.logical_not(low))
        def _():
            span(k, 2)
            span(k, 3)

        keep(k)

    def wait_relayed(k, side):
        view = (above, below)[side][k].at[pl.ds(side * (blocks + share), HB - share)]
        pltpu.make_async_copy(view, view, relay_done.at[k]).wait()

    def wait_up(k):
        @pl.when((me > 0) & (me != middle))
        def _():
            halo_up(k).wait_recv()

        @pl.when(me == middle)
        def _():
            direct(k, 0).wait_recv()
            wait_relayed(k, 0)

    def wait_down(k):
        @pl.when((me < peers - 1) & (me != middle - 1))
        def _():
            halo_down(k).wait_recv()

        @pl.when(me == middle - 1)
        def _():
            direct(k, 1).wait_recv()
            wait_relayed(k, 1)

    def wait_all(k):
        count = (peers - 1) * capacity
        view = arrived[k].at[pl.ds(0, count)]
        pltpu.make_async_copy(view, view, recv_sem.at[k]).wait()

    def wait_sends(k):
        count = (peers - 1) * capacity
        view = outgoing[k].at[pl.ds(0, count)]
        pltpu.make_async_copy(view, view, send_sem.at[k]).wait()

        @pl.when(me < peers - 1)
        def _():
            halo_up(k).wait_send()

        @pl.when(me > 0)
        def _():
            halo_down(k).wait_send()

        @pl.when(is_up_relay | is_down_relay)
        def _():
            pltpu.make_async_copy(relay[k], relay[k], relay_send.at[k]).wait()

    def norms(g, carry):
        total = jnp.zeros((block, 128), jnp.float32)
        for values, target in ((near_s, near_p), (far_s, far_p)):
            for c in range(values.shape[2] // 256):
                one = values[g, :, c * 256 : c * 256 + 128].astype(jnp.float32)
                two = values[g, :, c * 256 + 128 : c * 256 + 256].astype(jnp.float32)
                total = total + one * one + two * two
                low = jnp.where(even, one, pltpu.roll(two, short, 1))
                high = jnp.where(even, pltpu.roll(one, 128 - short, 1), two)
                target[g, 0:block, c * 128 : (c + 1) * 128] = low.astype(jnp.bfloat16)
                target[g, block:, c * 128 : (c + 1) * 128] = high.astype(jnp.bfloat16)
        squares = jnp.sum(total, axis=1, keepdims=True)
        scale = jnp.broadcast_to(lax.rsqrt(squares + 1e-06), (block, width))
        inv[g] = jnp.where(left, scale[:short], scale[short:])
        return carry

    def product(matrix, tiles):
        ordered = []
        for q in range(0, len(tiles), 4):
            ordered += [tiles[q], tiles[q + 2], tiles[q + 1], tiles[q + 3]]
        window = jnp.concatenate(ordered, axis=0)
        full = jnp.dot(matrix, window, preferred_element_type=jnp.float32)
        kept = jnp.where(left, full[:short], full[3 * short :])
        moved = jnp.where(left, full[short : 2 * short], full[2 * short : 3 * short])
        return kept + swap(moved)

    def near(k):
        def rows(first, count, source, shift):
            def one(i, carry):
                g = first + i
                tiles = [source[g + near_off[n, g] - shift] for n in range(near_count)]
                partial[g] = product(near_p[g], tiles)
                return carry

            lax.fori_loop(0, count, one, 0, unroll=True)

        def top():
            wait_up(k)
            rows(0, HB, above[k], 0)

        rows(HB, blocks - 2 * HB, own[k], HB)
        pl.when(low)(top)
        wait_down(k)
        rows(blocks - HB, HB, below[k], HB)
        pl.when(jnp.logical_not(low))(top)

    def far(k):
        depth, h = k // HALVES, k % HALVES

        def one(g, carry):
            tiles = [arrived[k][far_slot[j, g]] for j in range(far_count)]
            second = product(far_p[g], tiles)
            field = own[k][g].astype(jnp.float32)
            result = (partial[g] + second) * inv[g] - 0.2 * field
            if depth == 0:
                total = coef[0] * field
            else:
                result = 2.0 * result - own[k - HALVES][g].astype(jnp.float32)
                total = accum[h, g]
            total = total + coef[depth + 1] * result
            if depth < ORDER - 1:
                rounded = result.astype(jnp.bfloat16)
                own[k + HALVES][g] = rounded
                above[k + HALVES][HB + g] = rounded
                below[k + HALVES][g] = rounded
            if depth < ORDER - 1 or h == 0:
                accum[h, g] = total
            else:
                low, high = exchange(accum[0, g], total)
                out_ref[g, 0:short] = low.astype(jnp.bfloat16)
                out_ref[g, short:] = high.astype(jnp.bfloat16)
            return carry

        lax.fori_loop(0, blocks, one, 0, unroll=UNROLL)

    send_first()
    for k in range(HALVES):
        forward(k)
    for part in range(2):
        for copy in loads(part):
            copy.wait()
    lax.fori_loop(0, blocks, norms, 0, unroll=2)
    for k in range(stages):
        near(k)
        if 0 < k < stages - 1:
            forward(k + 1)
        wait_all(k)
        far(k)
        if k + HALVES < stages:
            send_all(k + HALVES)
    for k in range(stages):
        wait_sends(k)


def body(features, near_off, near_val, far_slot, far_val, send_blk):
    rows, width = features.shape
    blocks = near_off.shape[0]
    block = rows // blocks
    bands = lax.axis_size("band")
    subs = lax.axis_size("sub")
    capacity = send_blk.shape[2]
    slots = bands * subs * capacity
    short = block // HALVES
    stages = ORDER * HALVES
    near_wide = near_val.shape[1]
    far_wide = far_val.shape[1]
    vmem = pl.BlockSpec(memory_space=pltpu.VMEM)
    smem = pl.BlockSpec(memory_space=pltpu.SMEM)
    hbm = pl.BlockSpec(memory_space=pl.ANY)
    flops = 2 * ORDER * rows * (near_wide + far_wide) * width
    spectral = pl.pallas_call(
        functools.partial(kernel, bands, subs),
        out_shape=pltpu.VMEM((blocks, block, width), jnp.bfloat16),
        in_specs=[hbm, smem, smem, smem, hbm, hbm],
        out_specs=vmem,
        scratch_shapes=[
            pltpu.VMEM((blocks, block, width), jnp.bfloat16),
            pltpu.VMEM((blocks, block, near_wide), jnp.bfloat16),
            pltpu.VMEM((blocks, block, far_wide), jnp.bfloat16),
            pltpu.VMEM((blocks, HALVES * block, near_wide // HALVES), jnp.bfloat16),
            pltpu.VMEM((blocks, HALVES * block, far_wide // HALVES), jnp.bfloat16),
            [pltpu.VMEM((blocks, short, width), jnp.bfloat16)] * stages,
            [pltpu.VMEM((blocks + HB, short, width), jnp.bfloat16)] * stages,
            [pltpu.VMEM((blocks + HB, short, width), jnp.bfloat16)] * stages,
            [pltpu.VMEM((slots, short, width), jnp.bfloat16)] * stages,
            [pltpu.VMEM((slots, short, width), jnp.bfloat16)] * stages,
            pltpu.VMEM((blocks, short, width), jnp.float32),
            pltpu.VMEM((blocks, short, width), jnp.float32),
            pltpu.VMEM((HALVES, blocks, short, width), jnp.float32),
            pltpu.SemaphoreType.DMA,
            pltpu.SemaphoreType.DMA((2, CHUNKS)),
            pltpu.SemaphoreType.REGULAR((QUARTERS,)),
            pltpu.SemaphoreType.DMA((stages,)),
            pltpu.SemaphoreType.DMA((stages,)),
            pltpu.SemaphoreType.DMA((stages, 2)),
            pltpu.SemaphoreType.DMA((stages, 2)),
            [pltpu.VMEM((HB // RELAYS, short, width), jnp.bfloat16)] * stages,
            pltpu.SemaphoreType.DMA((stages,)),
            pltpu.SemaphoreType.DMA((stages,)),
            pltpu.SemaphoreType.DMA((stages,)),
        ],
        compiler_params=pltpu.CompilerParams(collective_id=0, has_side_effects=True),
        cost_estimate=pl.CostEstimate(
            flops=flops,
            bytes_accessed=2 * rows * (near_wide + far_wide + 2 * width),
            transcendentals=rows,
        ),
    )(
        features.reshape(blocks, block, width),
        near_off.T,
        far_slot.T,
        send_blk.transpose(0, 2, 1),
        near_val.reshape(blocks, block, near_wide),
        far_val.reshape(blocks, block, far_wide),
    )
    return spectral.reshape(rows, width)


def solution(mesh):
    placed = (
        P(("groups", "band", "sub"), None),
        P(("groups", "band", "sub"), None),
        P(("groups", "band", "sub"), None),
        P(("groups", "band", "sub"), None),
        P(("groups", "band", "sub"), None),
        P(("groups", "band", "sub"), None, None),
    )
    return jax.shard_map(
        body,
        mesh=mesh,
        in_specs=placed,
        out_specs=P(("groups", "band", "sub"), None),
        check_vma=False,
    )
```

```python
import functools
import math

import jax
import jax.numpy as jnp
from jax import lax
from jax.experimental import pallas as pl
from jax.experimental.pallas import tpu as pltpu
from jax.sharding import PartitionSpec as P

HB = 8
ORDER = 3
CHUNKS = 4
UNROLL = 12
HALVES = 2
QUARTERS = 4
RELAYS = 4
MESH = pl.DeviceIdType.MESH


def bessel_value(order, theta):
    total = 0.0
    for term in range(30):
        total += (theta / 2.0) ** (2 * term + order) / (
            math.factorial(term) * math.factorial(term + order)
        )
    return total


def coefficients(count):
    values = [bessel_value(0, 1.5)]
    for order in range(1, count + 1):
        values.append(2.0 * (-1.0) ** order * bessel_value(order, 1.5))
    return values


def kernel(
    bands,
    subs,
    feat_hbm,
    near_off_hbm,
    far_slot_hbm,
    send_blk_hbm,
    near_hbm,
    far_hbm,
    out_ref,
    near_off,
    far_slot,
    send_blk,
    feat_ref,
    near_s,
    far_s,
    near_p,
    far_p,
    own,
    above,
    below,
    outgoing,
    arrived,
    inv,
    partial,
    accum,
    table_sem,
    feat_sem,
    load_sem,
    ready,
    send_sem,
    recv_sem,
    halo_send,
    halo_recv,
    relay,
    relay_send,
    relay_recv,
):
    peers = bands * subs
    blocks, block, width = feat_ref.shape
    near_count = near_off.shape[0]
    far_count = far_slot.shape[0]
    capacity = send_blk.shape[1]
    me = lax.axis_index("band") * subs + lax.axis_index("sub")
    coef = coefficients(ORDER)
    step = blocks // CHUNKS
    short = block // HALVES
    stages = ORDER * HALVES
    left = lax.broadcasted_iota(jnp.int32, (short, width), 1) < width // 2
    even = lax.broadcasted_iota(jnp.int32, (block, 128), 1) % (2 * short) < short

    def swap(values):
        return pltpu.roll(values, width // 2, 1)

    def exchange(first, second):
        return jnp.where(left, first, swap(second)), jnp.where(left, swap(first), second)

    def where(peer):
        return {"band": peer // subs, "sub": peer % subs}

    def loads(part):
        source, target = ((near_hbm, near_s), (far_hbm, far_s))[part]
        return [
            pltpu.make_async_copy(
                source.at[pl.ds(c * step, step)],
                target.at[pl.ds(c * step, step)],
                load_sem.at[part, c],
            )
            for c in range(CHUNKS)
        ]

    barrier = pltpu.get_barrier_semaphore()

    def greet(peer, carry):
        pl.semaphore_signal(barrier, inc=1, device_id=where(peer), device_id_type=MESH)
        return carry

    lax.fori_loop(me + 1, peers, greet, 0)
    features = pltpu.make_async_copy(feat_hbm, feat_ref, feat_sem)
    tables = [
        pltpu.make_async_copy(source, target, table_sem.at[i])
        for i, (source, target) in enumerate(
            (
                (send_blk_hbm, send_blk),
                (near_off_hbm, near_off),
                (far_slot_hbm, far_slot),
            )
        )
    ]
    features.start()
    for copy in tables:
        copy.start()
    for part in range(2):
        for copy in loads(part):
            copy.start()

    @pl.when(me > 0)
    def _():
        pl.semaphore_wait(barrier, me)

    quarter = peers // QUARTERS

    def admit(peer, carry):
        pl.semaphore_signal(
            ready.at[me // quarter], inc=1, device_id=where(peer), device_id_type=MESH
        )
        return carry

    lax.fori_loop(0, me, admit, 0)
    features.wait()
    for copy in tables:
        copy.wait()

    def pack(g, carry):
        field = feat_ref[g].astype(jnp.float32)
        for h, packed in enumerate(exchange(field[:short], field[short:])):
            packed = packed.astype(jnp.bfloat16)
            own[h][g] = packed
            above[h][HB + g] = packed
            below[h][g] = packed
        return carry

    lax.fori_loop(0, blocks, pack, 0, unroll=4)

    @pl.when(me == 0)
    def _():
        for k in range(stages):
            above[k][0:HB] = jnp.zeros((HB, short, width), jnp.bfloat16)

    @pl.when(me == peers - 1)
    def _():
        for k in range(stages):
            below[k][blocks:] = jnp.zeros((HB, short, width), jnp.bfloat16)

    def halo_up(k):
        return pltpu.make_async_remote_copy(
            src_ref=own[k].at[pl.ds(blocks - HB, HB)],
            dst_ref=above[k].at[pl.ds(0, HB)],
            send_sem=halo_send.at[k, 0],
            recv_sem=halo_recv.at[k, 0],
            device_id=where((me + 1) % peers),
            device_id_type=MESH,
        )

    def halo_down(k):
        return pltpu.make_async_remote_copy(
            src_ref=own[k].at[pl.ds(0, HB)],
            dst_ref=below[k].at[pl.ds(blocks, HB)],
            send_sem=halo_send.at[k, 1],
            recv_sem=halo_recv.at[k, 1],
            device_id=where((me + peers - 1) % peers),
            device_id_type=MESH,
        )

    def await_ready(q):
        late = jnp.clip((q + 1) * quarter - 1 - me, 0, quarter)

        @pl.when(late > 0)
        def _():
            pl.semaphore_wait(ready.at[q], late)

    low = me < peers // 2

    def span(k, q):
        def one(j, carry):
            peer = q * quarter + j

            @pl.when(peer != me)
            def _():
                for c in range(capacity):
                    block_index = jnp.maximum(send_blk[0, c, peer], 0)
                    outgoing[k][peer * capacity + c] = own[k][block_index]
                pltpu.make_async_remote_copy(
                    src_ref=outgoing[k].at[pl.ds(peer * capacity, capacity)],
                    dst_ref=arrived[k].at[pl.ds(me * capacity, capacity)],
                    send_sem=send_sem.at[k],
                    recv_sem=recv_sem.at[k],
                    device_id=where(peer),
                    device_id_type=MESH,
                ).start()

            return carry

        lax.fori_loop(0, quarter, one, 0)

    middle = peers // 2
    share = HB // RELAYS
    up_relay = me < RELAYS
    down_relay = me >= peers - RELAYS

    def hand(k, side):
        @pl.when(me == middle - 1 + side)
        def _():
            for i in range(RELAYS):
                first = (1 - side) * (blocks - HB) + i * share
                pltpu.make_async_remote_copy(
                    src_ref=own[k].at[pl.ds(first, share)],
                    dst_ref=relay[k],
                    send_sem=halo_send.at[k, side],
                    recv_sem=relay_recv.at[k],
                    device_id=where(side * (peers - RELAYS) + i),
                    device_id_type=MESH,
                ).start()

    def forward(k):
        for side, mine in enumerate((up_relay, down_relay)):

            @pl.when(mine)
            def _():
                i = me - side * (peers - RELAYS)
                pltpu.make_async_copy(relay[k], relay[k], relay_recv.at[k]).wait()
                pltpu.make_async_remote_copy(
                    src_ref=relay[k],
                    dst_ref=(above, below)[side][k].at[
                        pl.ds(side * blocks + i * share, share)
                    ],
                    send_sem=relay_send.at[k],
                    recv_sem=halo_recv.at[k, side],
                    device_id=where(middle - side),
                    device_id_type=MESH,
                ).start()

    def send_down(k):
        @pl.when((me > 0) & (me != middle))
        def _():
            halo_down(k).start()

    def send_up(k):
        @pl.when((me < peers - 1) & (me != middle - 1))
        def _():
            halo_up(k).start()

    def keep(k):
        for c in range(capacity):
            block_index = jnp.maximum(send_blk[0, c, me], 0)
            arrived[k][me * capacity + c] = own[k][block_index]

    def across(k):
        @pl.when(low)
        def _():
            span(k, 2)
            span(k, 3)

        @pl.when(jnp.logical_not(low))
        def _():
            span(k, 0)
            span(k, 1)

    def within(k):
        @pl.when(low)
        def _():
            span(k, 0)
            span(k, 1)

        @pl.when(jnp.logical_not(low))
        def _():
            span(k, 2)
            span(k, 3)

    outer = (me < quarter) | (me >= peers - quarter)
    inner = jnp.logical_not(outer)

    def send_first():
        @pl.when(low)
        def _():
            await_ready(0)
            await_ready(1)
            for k in range(HALVES):
                hand(k, 0)
            for k in range(HALVES):
                send_down(k)
            within(0)
            await_ready(2)
            for k in range(HALVES):
                send_up(k)
            span(0, 2)
            await_ready(3)
            span(0, 3)
            within(1)
            across(1)

        @pl.when(jnp.logical_not(low))
        def _():
            for k in range(HALVES):
                send_down(k)
            across(0)
            await_ready(2)
            await_ready(3)
            for k in range(HALVES):
                hand(k, 1)
            for k in range(HALVES):
                send_up(k)
            within(0)
            across(1)
            within(1)

        for k in range(HALVES):
            keep(k)

    def send_all(k):
        hand(k, 0)
        hand(k, 1)
        send_down(k)
        send_up(k)
        across(k)
        within(k)
        keep(k)

    def wait_up(k):
        @pl.when(me > 0)
        def _():
            halo_up(k).wait_recv()

    def wait_down(k):
        @pl.when(me < peers - 1)
        def _():
            halo_down(k).wait_recv()

    def wait_all(k):
        count = (peers - 1) * capacity
        view = arrived[k].at[pl.ds(0, count)]
        pltpu.make_async_copy(view, view, recv_sem.at[k]).wait()

    def wait_sends(k):
        count = (peers - 1) * capacity
        view = outgoing[k].at[pl.ds(0, count)]
        pltpu.make_async_copy(view, view, send_sem.at[k]).wait()

        @pl.when(me < peers - 1)
        def _():
            halo_up(k).wait_send()

        @pl.when(me > 0)
        def _():
            halo_down(k).wait_send()

        @pl.when(up_relay | down_relay)
        def _():
            pltpu.make_async_copy(relay[k], relay[k], relay_send.at[k]).wait()

    def norms(g, carry):
        total = jnp.zeros((block, 128), jnp.float32)
        for values, target in ((near_s, near_p), (far_s, far_p)):
            for c in range(values.shape[2] // 256):
                one = values[g, :, c * 256 : c * 256 + 128].astype(jnp.float32)
                two = values[g, :, c * 256 + 128 : c * 256 + 256].astype(jnp.float32)
                total = total + one * one + two * two
                low = jnp.where(even, one, pltpu.roll(two, short, 1))
                high = jnp.where(even, pltpu.roll(one, 128 - short, 1), two)
                target[g, 0:block, c * 128 : (c + 1) * 128] = low.astype(jnp.bfloat16)
                target[g, block:, c * 128 : (c + 1) * 128] = high.astype(jnp.bfloat16)
        squares = jnp.sum(total, axis=1, keepdims=True)
        scale = jnp.broadcast_to(lax.rsqrt(squares + 1e-06), (block, width))
        inv[g] = jnp.where(left, scale[:short], scale[short:])
        return carry

    def product(matrix, tiles):
        ordered = []
        for q in range(0, len(tiles), 4):
            ordered += [tiles[q], tiles[q + 2], tiles[q + 1], tiles[q + 3]]
        window = jnp.concatenate(ordered, axis=0)
        full = jnp.dot(matrix, window, preferred_element_type=jnp.float32)
        kept = jnp.where(left, full[:short], full[3 * short :])
        moved = jnp.where(left, full[short : 2 * short], full[2 * short : 3 * short])
        return kept + swap(moved)

    def near(k):
        def rows(first, count, source, shift):
            def one(i, carry):
                g = first + i
                tiles = [source[g + near_off[n, g] - shift] for n in range(near_count)]
                partial[g] = product(near_p[g], tiles)
                return carry

            lax.fori_loop(0, count, one, 0, unroll=True)

        def top():
            wait_up(k)
            rows(0, HB, above[k], 0)

        rows(HB, blocks - 2 * HB, own[k], HB)
        pl.when(low)(top)
        wait_down(k)
        rows(blocks - HB, HB, below[k], HB)
        pl.when(jnp.logical_not(low))(top)

    def far(k):
        depth, h = k // HALVES, k % HALVES

        def one(g, carry):
            tiles = [arrived[k][far_slot[j, g]] for j in range(far_count)]
            second = product(far_p[g], tiles)
            field = own[k][g].astype(jnp.float32)
            result = (partial[g] + second) * inv[g] - 0.2 * field
            if depth == 0:
                total = coef[0] * field
            else:
                result = 2.0 * result - own[k - HALVES][g].astype(jnp.float32)
                total = accum[h, g]
            total = total + coef[depth + 1] * result
            if depth < ORDER - 1:
                rounded = result.astype(jnp.bfloat16)
                own[k + HALVES][g] = rounded
                above[k + HALVES][HB + g] = rounded
                below[k + HALVES][g] = rounded
            if depth < ORDER - 1 or h == 0:
                accum[h, g] = total
            else:
                low, high = exchange(accum[0, g], total)
                out_ref[g, 0:short] = low.astype(jnp.bfloat16)
                out_ref[g, short:] = high.astype(jnp.bfloat16)
            return carry

        lax.fori_loop(0, blocks, one, 0, unroll=UNROLL)

    send_first()
    for k in range(HALVES):
        forward(k)
    for part in range(2):
        for copy in loads(part):
            copy.wait()
    lax.fori_loop(0, blocks, norms, 0, unroll=2)
    for k in range(stages):
        near(k)
        if 0 < k < stages - 1:
            forward(k + 1)
        wait_all(k)
        far(k)
        if k + HALVES < stages:
            send_all(k + HALVES)
    for k in range(stages):
        wait_sends(k)


def body(features, near_off, near_val, far_slot, far_val, send_blk):
    rows, width = features.shape
    blocks = near_off.shape[0]
    block = rows // blocks
    bands = lax.axis_size("band")
    subs = lax.axis_size("sub")
    capacity = send_blk.shape[2]
    slots = bands * subs * capacity
    short = block // HALVES
    stages = ORDER * HALVES
    near_wide = near_val.shape[1]
    far_wide = far_val.shape[1]
    vmem = pl.BlockSpec(memory_space=pltpu.VMEM)
    hbm = pl.BlockSpec(memory_space=pl.ANY)
    flops = 2 * ORDER * rows * (near_wide + far_wide) * width
    spectral = pl.pallas_call(
        functools.partial(kernel, bands, subs),
        out_shape=pltpu.VMEM((blocks, block, width), jnp.bfloat16),
        in_specs=[hbm] * 6,
        out_specs=vmem,
        scratch_shapes=[
            pltpu.SMEM((near_wide // block, blocks), jnp.int32),
            pltpu.SMEM((far_wide // block, blocks), jnp.int32),
            pltpu.SMEM((1, capacity, bands * subs), jnp.int32),
            pltpu.VMEM((blocks, block, width), jnp.bfloat16),
            pltpu.VMEM((blocks, block, near_wide), jnp.bfloat16),
            pltpu.VMEM((blocks, block, far_wide), jnp.bfloat16),
            pltpu.VMEM((blocks, HALVES * block, near_wide // HALVES), jnp.bfloat16),
            pltpu.VMEM((blocks, HALVES * block, far_wide // HALVES), jnp.bfloat16),
            [pltpu.VMEM((blocks, short, width), jnp.bfloat16)] * stages,
            [pltpu.VMEM((blocks + HB, short, width), jnp.bfloat16)] * stages,
            [pltpu.VMEM((blocks + HB, short, width), jnp.bfloat16)] * stages,
            [pltpu.VMEM((slots, short, width), jnp.bfloat16)] * stages,
            [pltpu.VMEM((slots, short, width), jnp.bfloat16)] * stages,
            pltpu.VMEM((blocks, short, width), jnp.float32),
            pltpu.VMEM((blocks, short, width), jnp.float32),
            pltpu.VMEM((HALVES, blocks, short, width), jnp.float32),
            pltpu.SemaphoreType.DMA((3,)),
            pltpu.SemaphoreType.DMA,
            pltpu.SemaphoreType.DMA((2, CHUNKS)),
            pltpu.SemaphoreType.REGULAR((QUARTERS,)),
            pltpu.SemaphoreType.DMA((stages,)),
            pltpu.SemaphoreType.DMA((stages,)),
            pltpu.SemaphoreType.DMA((stages, 2)),
            pltpu.SemaphoreType.DMA((stages, 2)),
            [pltpu.VMEM((HB // RELAYS, short, width), jnp.bfloat16)] * stages,
            pltpu.SemaphoreType.DMA((stages,)),
            pltpu.SemaphoreType.DMA((stages,)),
        ],
        compiler_params=pltpu.CompilerParams(collective_id=0, has_side_effects=True),
        cost_estimate=pl.CostEstimate(
            flops=flops,
            bytes_accessed=2 * rows * (near_wide + far_wide + 2 * width),
            transcendentals=rows,
        ),
    )(
        features.reshape(blocks, block, width),
        near_off.T,
        far_slot.T,
        send_blk.transpose(0, 2, 1),
        near_val.reshape(blocks, block, near_wide),
        far_val.reshape(blocks, block, far_wide),
    )
    return spectral.reshape(rows, width)


def solution(mesh):
    placed = (
        P(("groups", "band", "sub"), None),
        P(("groups", "band", "sub"), None),
        P(("groups", "band", "sub"), None),
        P(("groups", "band", "sub"), None),
        P(("groups", "band", "sub"), None),
        P(("groups", "band", "sub"), None, None),
    )
    return jax.shard_map(
        body,
        mesh=mesh,
        in_specs=placed,
        out_specs=P(("groups", "band", "sub"), None),
        check_vma=False,
    )
```

```python
import functools
import math

import jax
import jax.numpy as jnp
from jax import lax
from jax.experimental import pallas as pl
from jax.experimental.pallas import tpu as pltpu
from jax.sharding import PartitionSpec as P

HB = 8
ORDER = 3
CHUNKS = 4
UNROLL = 24
HALVES = 2
QUARTERS = 4
RELAYS = 4
MESH = pl.DeviceIdType.MESH


def bessel_value(order, theta):
    total = 0.0
    for term in range(30):
        total += (theta / 2.0) ** (2 * term + order) / (
            math.factorial(term) * math.factorial(term + order)
        )
    return total


def coefficients(count):
    values = [bessel_value(0, 1.5)]
    for order in range(1, count + 1):
        values.append(2.0 * (-1.0) ** order * bessel_value(order, 1.5))
    return values


def kernel(
    bands,
    subs,
    feat_hbm,
    near_off_hbm,
    far_slot_hbm,
    send_blk_hbm,
    near_hbm,
    far_hbm,
    out_ref,
    near_off,
    far_slot,
    send_blk,
    feat_ref,
    near_s,
    far_s,
    near_p,
    far_p,
    own,
    above,
    below,
    outgoing,
    arrived,
    inv,
    partial,
    accum,
    table_sem,
    feat_sem,
    load_sem,
    ready,
    send_sem,
    recv_sem,
    halo_send,
    halo_recv,
    relay,
    relay_send,
    relay_recv,
):
    peers = bands * subs
    blocks, block, width = feat_ref.shape
    near_count = near_off.shape[0]
    far_count = far_slot.shape[0]
    capacity = send_blk.shape[1]
    me = lax.axis_index("band") * subs + lax.axis_index("sub")
    coef = coefficients(ORDER)
    step = blocks // CHUNKS
    short = block // HALVES
    stages = ORDER * HALVES
    left = lax.broadcasted_iota(jnp.int32, (short, width), 1) < width // 2
    even = lax.broadcasted_iota(jnp.int32, (block, 128), 1) % (2 * short) < short

    def swap(values):
        return pltpu.roll(values, width // 2, 1)

    def exchange(first, second):
        return jnp.where(left, first, swap(second)), jnp.where(left, swap(first), second)

    def where(peer):
        return {"band": peer // subs, "sub": peer % subs}

    def loads(part):
        source, target = ((near_hbm, near_s), (far_hbm, far_s))[part]
        return [
            pltpu.make_async_copy(
                source.at[pl.ds(c * step, step)],
                target.at[pl.ds(c * step, step)],
                load_sem.at[part, c],
            )
            for c in range(CHUNKS)
        ]

    barrier = pltpu.get_barrier_semaphore()

    def greet(peer, carry):
        pl.semaphore_signal(barrier, inc=1, device_id=where(peer), device_id_type=MESH)
        return carry

    lax.fori_loop(me + 1, peers, greet, 0)
    features = pltpu.make_async_copy(feat_hbm, feat_ref, feat_sem)
    tables = [
        pltpu.make_async_copy(source, target, table_sem.at[i])
        for i, (source, target) in enumerate(
            (
                (send_blk_hbm, send_blk),
                (near_off_hbm, near_off),
                (far_slot_hbm, far_slot),
            )
        )
    ]
    features.start()
    for copy in tables:
        copy.start()
    for part in range(2):
        for copy in loads(part):
            copy.start()

    @pl.when(me > 0)
    def _():
        pl.semaphore_wait(barrier, me)

    quarter = peers // QUARTERS

    def admit(peer, carry):
        pl.semaphore_signal(
            ready.at[me // quarter], inc=1, device_id=where(peer), device_id_type=MESH
        )
        return carry

    lax.fori_loop(0, me, admit, 0)
    features.wait()
    for copy in tables:
        copy.wait()

    def pack(g, carry):
        field = feat_ref[g].astype(jnp.float32)
        for h, packed in enumerate(exchange(field[:short], field[short:])):
            packed = packed.astype(jnp.bfloat16)
            own[h][g] = packed
            above[h][HB + g] = packed
            below[h][g] = packed
        return carry

    lax.fori_loop(0, blocks, pack, 0, unroll=4)

    @pl.when(me == 0)
    def _():
        for k in range(stages):
            above[k][0:HB] = jnp.zeros((HB, short, width), jnp.bfloat16)

    @pl.when(me == peers - 1)
    def _():
        for k in range(stages):
            below[k][blocks:] = jnp.zeros((HB, short, width), jnp.bfloat16)

    def halo_up(k):
        return pltpu.make_async_remote_copy(
            src_ref=own[k].at[pl.ds(blocks - HB, HB)],
            dst_ref=above[k].at[pl.ds(0, HB)],
            send_sem=halo_send.at[k, 0],
            recv_sem=halo_recv.at[k, 0],
            device_id=where((me + 1) % peers),
            device_id_type=MESH,
        )

    def halo_down(k):
        return pltpu.make_async_remote_copy(
            src_ref=own[k].at[pl.ds(0, HB)],
            dst_ref=below[k].at[pl.ds(blocks, HB)],
            send_sem=halo_send.at[k, 1],
            recv_sem=halo_recv.at[k, 1],
            device_id=where((me + peers - 1) % peers),
            device_id_type=MESH,
        )

    def await_ready(q):
        late = jnp.clip((q + 1) * quarter - 1 - me, 0, quarter)

        @pl.when(late > 0)
        def _():
            pl.semaphore_wait(ready.at[q], late)

    low = me < peers // 2

    def span(k, q):
        def one(j, carry):
            peer = q * quarter + j

            @pl.when(peer != me)
            def _():
                for c in range(capacity):
                    block_index = jnp.maximum(send_blk[0, c, peer], 0)
                    outgoing[k][peer * capacity + c] = own[k][block_index]
                pltpu.make_async_remote_copy(
                    src_ref=outgoing[k].at[pl.ds(peer * capacity, capacity)],
                    dst_ref=arrived[k].at[pl.ds(me * capacity, capacity)],
                    send_sem=send_sem.at[k],
                    recv_sem=recv_sem.at[k],
                    device_id=where(peer),
                    device_id_type=MESH,
                ).start()

            return carry

        lax.fori_loop(0, quarter, one, 0)

    middle = peers // 2
    share = HB // RELAYS
    up_relay = me < RELAYS
    down_relay = me >= peers - RELAYS

    def hand(k, side):
        @pl.when(me == middle - 1 + side)
        def _():
            for i in range(RELAYS):
                first = (1 - side) * (blocks - HB) + i * share
                pltpu.make_async_remote_copy(
                    src_ref=own[k].at[pl.ds(first, share)],
                    dst_ref=relay[k],
                    send_sem=halo_send.at[k, side],
                    recv_sem=relay_recv.at[k],
                    device_id=where(side * (peers - RELAYS) + i),
                    device_id_type=MESH,
                ).start()

    def forward(k):
        for side, mine in enumerate((up_relay, down_relay)):

            @pl.when(mine)
            def _():
                i = me - side * (peers - RELAYS)
                pltpu.make_async_copy(relay[k], relay[k], relay_recv.at[k]).wait()
                pltpu.make_async_remote_copy(
                    src_ref=relay[k],
                    dst_ref=(above, below)[side][k].at[
                        pl.ds(side * blocks + i * share, share)
                    ],
                    send_sem=relay_send.at[k],
                    recv_sem=halo_recv.at[k, side],
                    device_id=where(middle - side),
                    device_id_type=MESH,
                ).start()

    def send_down(k):
        @pl.when((me > 0) & (me != middle))
        def _():
            halo_down(k).start()

    def send_up(k):
        @pl.when((me < peers - 1) & (me != middle - 1))
        def _():
            halo_up(k).start()

    def keep(k):
        for c in range(capacity):
            block_index = jnp.maximum(send_blk[0, c, me], 0)
            arrived[k][me * capacity + c] = own[k][block_index]

    def across(k):
        @pl.when(low)
        def _():
            span(k, 2)
            span(k, 3)

        @pl.when(jnp.logical_not(low))
        def _():
            span(k, 0)
            span(k, 1)

    def within(k):
        @pl.when(low)
        def _():
            span(k, 0)
            span(k, 1)

        @pl.when(jnp.logical_not(low))
        def _():
            span(k, 2)
            span(k, 3)

    outer = (me < quarter) | (me >= peers - quarter)
    inner = jnp.logical_not(outer)

    def send_first():
        @pl.when(low)
        def _():
            await_ready(0)
            await_ready(1)
            for k in range(HALVES):
                hand(k, 0)
            for k in range(HALVES):
                send_down(k)
            within(0)
            await_ready(2)
            for k in range(HALVES):
                send_up(k)
            span(0, 2)
            await_ready(3)
            span(0, 3)
            within(1)
            across(1)

        @pl.when(jnp.logical_not(low))
        def _():
            for k in range(HALVES):
                send_down(k)
            across(0)
            await_ready(2)
            await_ready(3)
            for k in range(HALVES):
                hand(k, 1)
            for k in range(HALVES):
                send_up(k)
            within(0)
            across(1)
            within(1)

        for k in range(HALVES):
            keep(k)

    def send_all(k):
        hand(k, 0)
        hand(k, 1)
        send_down(k)
        send_up(k)
        across(k)
        within(k)
        keep(k)

    def wait_up(k):
        @pl.when(me > 0)
        def _():
            halo_up(k).wait_recv()

    def wait_down(k):
        @pl.when(me < peers - 1)
        def _():
            halo_down(k).wait_recv()

    def wait_all(k):
        count = (peers - 1) * capacity
        view = arrived[k].at[pl.ds(0, count)]
        pltpu.make_async_copy(view, view, recv_sem.at[k]).wait()

    def wait_sends(k):
        count = (peers - 1) * capacity
        view = outgoing[k].at[pl.ds(0, count)]
        pltpu.make_async_copy(view, view, send_sem.at[k]).wait()

        @pl.when(me < peers - 1)
        def _():
            halo_up(k).wait_send()

        @pl.when(me > 0)
        def _():
            halo_down(k).wait_send()

        @pl.when(up_relay | down_relay)
        def _():
            pltpu.make_async_copy(relay[k], relay[k], relay_send.at[k]).wait()

    def norms(g, carry):
        total = jnp.zeros((block, 128), jnp.float32)
        for values, target in ((near_s, near_p), (far_s, far_p)):
            for c in range(values.shape[2] // 256):
                one = values[g, :, c * 256 : c * 256 + 128].astype(jnp.float32)
                two = values[g, :, c * 256 + 128 : c * 256 + 256].astype(jnp.float32)
                total = total + one * one + two * two
                low = jnp.where(even, one, pltpu.roll(two, short, 1))
                high = jnp.where(even, pltpu.roll(one, 128 - short, 1), two)
                target[g, 0:block, c * 128 : (c + 1) * 128] = low.astype(jnp.bfloat16)
                target[g, block:, c * 128 : (c + 1) * 128] = high.astype(jnp.bfloat16)
        squares = jnp.sum(total, axis=1, keepdims=True)
        scale = jnp.broadcast_to(lax.rsqrt(squares + 1e-06), (block, width))
        inv[g] = jnp.where(left, scale[:short], scale[short:])
        return carry

    def product(matrix, tiles):
        ordered = []
        for q in range(0, len(tiles), 4):
            ordered += [tiles[q], tiles[q + 2], tiles[q + 1], tiles[q + 3]]
        window = jnp.concatenate(ordered, axis=0)
        full = jnp.dot(matrix, window, preferred_element_type=jnp.float32)
        kept = jnp.where(left, full[:short], full[3 * short :])
        moved = jnp.where(left, full[short : 2 * short], full[2 * short : 3 * short])
        return kept + swap(moved)

    def near(k):
        def rows(first, count, source, shift):
            def one(i, carry):
                g = first + i
                tiles = [source[g + near_off[n, g] - shift] for n in range(near_count)]
                partial[g] = product(near_p[g], tiles)
                return carry

            lax.fori_loop(0, count, one, 0, unroll=True)

        def top():
            wait_up(k)
            rows(0, HB, above[k], 0)

        rows(HB, blocks - 2 * HB, own[k], HB)
        pl.when(low)(top)
        wait_down(k)
        rows(blocks - HB, HB, below[k], HB)
        pl.when(jnp.logical_not(low))(top)

    def far(k):
        depth, h = k // HALVES, k % HALVES

        def one(g, carry):
            tiles = [arrived[k][far_slot[j, g]] for j in range(far_count)]
            second = product(far_p[g], tiles)
            field = own[k][g].astype(jnp.float32)
            result = (partial[g] + second) * inv[g] - 0.2 * field
            if depth == 0:
                total = coef[0] * field
            else:
                result = 2.0 * result - own[k - HALVES][g].astype(jnp.float32)
                total = accum[h, g]
            total = total + coef[depth + 1] * result
            if depth < ORDER - 1:
                rounded = result.astype(jnp.bfloat16)
                own[k + HALVES][g] = rounded
                above[k + HALVES][HB + g] = rounded
                below[k + HALVES][g] = rounded
            if depth < ORDER - 1 or h == 0:
                accum[h, g] = total
            else:
                low, high = exchange(accum[0, g], total)
                out_ref[g, 0:short] = low.astype(jnp.bfloat16)
                out_ref[g, short:] = high.astype(jnp.bfloat16)
            return carry

        lax.fori_loop(0, blocks, one, 0, unroll=UNROLL)

    send_first()
    for k in range(HALVES):
        forward(k)
    for part in range(2):
        for copy in loads(part):
            copy.wait()
    lax.fori_loop(0, blocks, norms, 0, unroll=2)
    for k in range(stages):
        near(k)
        wait_all(k)
        if 0 < k < stages - 1:
            forward(k + 1)
        far(k)
        if k + HALVES < stages:
            send_all(k + HALVES)
    for k in range(stages):
        wait_sends(k)


def body(features, near_off, near_val, far_slot, far_val, send_blk):
    rows, width = features.shape
    blocks = near_off.shape[0]
    block = rows // blocks
    bands = lax.axis_size("band")
    subs = lax.axis_size("sub")
    capacity = send_blk.shape[2]
    slots = bands * subs * capacity
    short = block // HALVES
    stages = ORDER * HALVES
    near_wide = near_val.shape[1]
    far_wide = far_val.shape[1]
    vmem = pl.BlockSpec(memory_space=pltpu.VMEM)
    hbm = pl.BlockSpec(memory_space=pl.ANY)
    flops = 2 * ORDER * rows * (near_wide + far_wide) * width
    spectral = pl.pallas_call(
        functools.partial(kernel, bands, subs),
        out_shape=pltpu.VMEM((blocks, block, width), jnp.bfloat16),
        in_specs=[hbm] * 6,
        out_specs=vmem,
        scratch_shapes=[
            pltpu.SMEM((near_wide // block, blocks), jnp.int32),
            pltpu.SMEM((far_wide // block, blocks), jnp.int32),
            pltpu.SMEM((1, capacity, bands * subs), jnp.int32),
            pltpu.VMEM((blocks, block, width), jnp.bfloat16),
            pltpu.VMEM((blocks, block, near_wide), jnp.bfloat16),
            pltpu.VMEM((blocks, block, far_wide), jnp.bfloat16),
            pltpu.VMEM((blocks, HALVES * block, near_wide // HALVES), jnp.bfloat16),
            pltpu.VMEM((blocks, HALVES * block, far_wide // HALVES), jnp.bfloat16),
            [pltpu.VMEM((blocks, short, width), jnp.bfloat16)] * stages,
            [pltpu.VMEM((blocks + HB, short, width), jnp.bfloat16)] * stages,
            [pltpu.VMEM((blocks + HB, short, width), jnp.bfloat16)] * stages,
            [pltpu.VMEM((slots, short, width), jnp.bfloat16)] * stages,
            [pltpu.VMEM((slots, short, width), jnp.bfloat16)] * stages,
            pltpu.VMEM((blocks, short, width), jnp.float32),
            pltpu.VMEM((blocks, short, width), jnp.float32),
            pltpu.VMEM((HALVES, blocks, short, width), jnp.float32),
            pltpu.SemaphoreType.DMA((3,)),
            pltpu.SemaphoreType.DMA,
            pltpu.SemaphoreType.DMA((2, CHUNKS)),
            pltpu.SemaphoreType.REGULAR((QUARTERS,)),
            pltpu.SemaphoreType.DMA((stages,)),
            pltpu.SemaphoreType.DMA((stages,)),
            pltpu.SemaphoreType.DMA((stages, 2)),
            pltpu.SemaphoreType.DMA((stages, 2)),
            [pltpu.VMEM((HB // RELAYS, short, width), jnp.bfloat16)] * stages,
            pltpu.SemaphoreType.DMA((stages,)),
            pltpu.SemaphoreType.DMA((stages,)),
        ],
        compiler_params=pltpu.CompilerParams(collective_id=0, has_side_effects=True),
        cost_estimate=pl.CostEstimate(
            flops=flops,
            bytes_accessed=2 * rows * (near_wide + far_wide + 2 * width),
            transcendentals=rows,
        ),
    )(
        features.reshape(blocks, block, width),
        near_off.T,
        far_slot.T,
        send_blk.transpose(0, 2, 1),
        near_val.reshape(blocks, block, near_wide),
        far_val.reshape(blocks, block, far_wide),
    )
    return spectral.reshape(rows, width)


def solution(mesh):
    placed = (
        P(("groups", "band", "sub"), None),
        P(("groups", "band", "sub"), None),
        P(("groups", "band", "sub"), None),
        P(("groups", "band", "sub"), None),
        P(("groups", "band", "sub"), None),
        P(("groups", "band", "sub"), None, None),
    )
    return jax.shard_map(
        body,
        mesh=mesh,
        in_specs=placed,
        out_specs=P(("groups", "band", "sub"), None),
        check_vma=False,
    )
```
